512 devices in a mesh: user: 64 (over y, z), item: 8 (over x, core).
Axes of the slice: x: 4, y: 4, z: 16, core: 2. Of those that a mesh axis runs over, the one named last changes fastest.
Arguments:
- user_factors: bfloat16 [65536, 256], P('user'), may hold values from -0.3984375 to 0.3984375
- item_panels: float32 [524288, 256], P(('user', 'item')), may hold values from -6 to 6
- ratings: bfloat16 [3, 1536, 1024, 128], P(None, 'user', 'item'), may hold values from -6 to 6
- tile_ids: int32 [3, 1536, 8], P(None, 'user', 'item'), may hold values from 0 to 63, as said below
- tile_count: int32 [3, 64, 8], P(None, 'user', 'item'), may hold values from 6 to 24, as said below
Outputs:
- panels_out: float32 [524288, 256], P(('user', 'item'))
- user_grad: float32 [65536, 256], P(('user', 'item'))
The draws below stay inside these ranges and needn't reach their ends.
Inputs may be any that keep to these rules, and one draw needn't show every extreme that they name: `tile_ids`: the first 24 entries of each user block's list for a group and step are distinct tiles of the block. `tile_count`: in every step some user block and group has all 24 slots live.
All inputs are finite; a program needn't handle non-finite values.
Results may differ from the reference program's by a relative error of at most 0.0013.
Values sent between devices are 32-bit elements; how exact they have to be, the bound alone decides.
No kernel may reach another device: no remote copies, remote signals or barrier semaphores. Data moves between devices by JAX's collectives and lax.ppermute only.
A program may use at most 64 MiB of HBM per device.

```python
import jax
import jax.numpy as jnp
from jax import lax

R = 256
TILE = 128
USER_ROWS = 1024
PANEL = 1024
STEPS = 3
TILES_BLOCK = 64
SLOTS = 24
CYCLE = 64
GROUPS = 8
USERS = 65536
ITEMS = 524288
SLOT_ROWS = 1536
GROUP_ROWS = 1024


def draw_tile_ids(key, part):
    keys = jax.random.split(jax.random.fold_in(key, 11), STEPS * CYCLE * GROUPS)
    chosen = jax.vmap(lambda one_key: jax.random.permutation(one_key, TILES_BLOCK)[:SLOTS])(keys)
    chosen = chosen.reshape(STEPS, CYCLE, GROUPS, SLOTS).transpose(0, 1, 3, 2)
    return chosen.reshape(STEPS, CYCLE * SLOTS, GROUPS).astype(jnp.int32)


def draw_tile_count(key, part):
    base = jax.random.randint(jax.random.fold_in(key, 21), (STEPS, CYCLE * GROUPS), (SLOTS + 3) // 4, SLOTS + 1)
    fullest = jax.random.randint(jax.random.fold_in(key, 22), (STEPS, 1), 0, CYCLE * GROUPS)
    places = jnp.arange(CYCLE * GROUPS)[None, :]
    counts = jnp.where(places == fullest, SLOTS, base)
    return counts.reshape(STEPS, CYCLE, GROUPS).astype(jnp.int32)


def block_levels(own_key, shape, cuts, least, top_value):
    loudness = 1.0
    for position, blocks in cuts:
        heights = jax.random.uniform(jax.random.fold_in(jax.random.fold_in(own_key, 6), position), (blocks,), jnp.float32, least / len(cuts), top_value / len(cuts))
        loudness = loudness * jnp.repeat(jnp.exp(heights), shape[position] // blocks).reshape((-1,) + (1,) * (len(shape) - 1 - position))
    return loudness


def normal_values(own_key, extent, deviation, reach, shards=(), held_as=jnp.bfloat16):
    factor_of = block_levels(own_key, extent, shards, -0.22, 0.18) if shards else 1.0
    result = jax.random.normal(own_key, extent, jnp.float32) * deviation * factor_of
    return jnp.minimum(jnp.maximum(result, -reach), reach).astype(held_as)


def setup_inputs(seed: int = 0) -> dict:
    splits = jax.random.split(jax.random.key(seed), 6)
    return {
        "user_factors": normal_values(splits[0], (USERS, R), 0.0625, 0.3984375, ((0, 64),)),
        "item_panels": normal_values(splits[1], (ITEMS, R), 1.0, 6.0, ((0, 512),), jnp.float32),
        "ratings": normal_values(splits[2], (STEPS, SLOT_ROWS, GROUP_ROWS, TILE), 1.0, 6.0, ((1, 64), (2, 8))),
        "tile_ids": draw_tile_ids(jax.random.fold_in(splits[5], 71), 0),
        "tile_count": draw_tile_count(jax.random.fold_in(splits[5], 71), 0),
    }


learn_rate = 0.05
weight_decay = 0.02
user_scale = 1.0 / 64.0


def update_block(user_block, item_block, rating_tiles, tile_list, live_count):
    row_tiles = user_block.shape[0] // TILE
    col_tiles = item_block.shape[0] // TILE
    row_index = tile_list // col_tiles
    col_index = tile_list % col_tiles
    user_tiles = user_block.astype(jnp.float32).reshape(row_tiles, TILE, R)[row_index]
    item_tiles = item_block.astype(jnp.bfloat16).astype(jnp.float32).reshape(col_tiles, TILE, R)[col_index]
    predicted = jnp.einsum("kir,kjr->kij", user_tiles, item_tiles, precision=lax.Precision.HIGHEST)
    live_mask = (jnp.arange(tile_list.shape[0]) < live_count).astype(jnp.float32)
    residual = ((predicted - rating_tiles.astype(jnp.float32)) * live_mask[:, None, None]).astype(jnp.bfloat16).astype(jnp.float32)
    item_parts = jnp.einsum("kij,kir->kjr", residual, user_tiles, precision=lax.Precision.HIGHEST)
    user_parts = jnp.einsum("kij,kjr->kir", residual, item_tiles, precision=lax.Precision.HIGHEST)
    col_pick = (col_index[:, None] == jnp.arange(col_tiles)[None, :]).astype(jnp.float32)
    row_pick = (row_index[:, None] == jnp.arange(row_tiles)[None, :]).astype(jnp.float32)
    item_grad = jnp.einsum("kc,kjr->cjr", col_pick, item_parts, precision=lax.Precision.HIGHEST).reshape(-1, R)
    user_grad = jnp.einsum("ka,kir->air", row_pick, user_parts, precision=lax.Precision.HIGHEST).reshape(-1, R)
    new_block = item_block - learn_rate * (item_grad + weight_decay * item_block)
    return new_block, user_scale * user_grad


def reference(user_factors, item_panels, ratings, tile_ids, tile_count):
    user_blocks = user_factors.reshape(CYCLE, USER_ROWS, R)
    panels = item_panels.reshape(CYCLE, GROUPS, PANEL, R)
    rating_all = ratings.reshape(STEPS, CYCLE, SLOTS, GROUPS, TILE, TILE)
    list_all = tile_ids.reshape(STEPS, CYCLE, SLOTS, GROUPS)
    gradient = jnp.zeros((CYCLE, USER_ROWS, R), jnp.float32)

    def per_user(packed):
        user_block, group_panels, group_ratings, group_lists, group_counts = packed
        new_panels, user_parts = jax.vmap(update_block, in_axes=(None, 0, 1, 1, 0))(
            user_block, group_panels, group_ratings, group_lists, group_counts)
        return new_panels, jnp.sum(user_parts, axis=0)

    for step_index in range(STEPS):
        if step_index > 0:
            panels = jnp.roll(panels, 1, axis=0)
        panels, user_parts = lax.map(per_user, (user_blocks, panels, rating_all[step_index],
                                                list_all[step_index], tile_count[step_index]))
        gradient = gradient + user_parts
    return panels.reshape(ITEMS, R), gradient.reshape(USERS, R)
```

```python
import functools

import jax
import jax.numpy as jnp
from jax import lax
from jax.experimental import pallas as pl
from jax.experimental.pallas import tpu as pltpu
from jax.sharding import PartitionSpec as P

R = 256
TILE = 128
STEPS = 3
ROW_TILES = 8
COL_TILES = 8
SLOTS = 24
WIDE = 2 * TILE


learn_rate = 0.05
weight_decay = 0.02
user_scale = 1.0 / 64.0

CORE_GROUPS = [[0, 2, 4, 6], [1, 3, 5, 7]]


def passed_along(value, axis, steps):
    count = lax.axis_size(axis)
    pairs = [(source, (source + steps) % count) for source in range(count)]
    return lax.ppermute(value, axis, pairs)


def chunk_body(step, part, parts, has_total, split, *refs):
    refs = list(refs)
    ids_ref, count_ref, users_ref, panel_ref, rating_ref = refs[:5]
    refs = refs[5:]
    if has_total:
        total_ref = refs.pop(0)
    if step == STEPS - 1 and part > 0:
        refs.pop(0)
    new_ref = refs.pop(0)
    if split:
        mine_ref, theirs_ref = refs.pop(0), refs.pop(0)
    else:
        out_ref = refs.pop(0)
    slot_ref, residual, rounded = refs[:3]
    if split:
        out_ref = refs[3]
    columns = COL_TILES * TILE // parts

    def clear(index, carry):
        slot_ref[index] = -1
        return carry

    lax.fori_loop(0, ROW_TILES * COL_TILES, clear, 0, unroll=True)
    live_count = count_ref[step, 0]
    for slot in range(SLOTS):
        slot_ref[ids_ref[step, slot]] = jnp.where(slot < live_count, slot, -1)

    rounded[...] = panel_ref[...].astype(jnp.bfloat16)
    contract_last = (((1,), (1,)), ((), ()))
    contract_first = (((0,), (0,)), ((), ()))
    for wide in range(columns // WIDE):
        cols = slice(wide * WIDE, (wide + 1) * WIDE)
        for block in range(ROW_TILES // 2):
            rows = slice(block * WIDE, (block + 1) * WIDE)
            predicted = lax.dot_general(
                users_ref[rows, :], rounded[cols, :], contract_last, preferred_element_type=jnp.float32
            )
            for down in range(2):
                for across in range(2):
                    tile_row = block * 2 + down
                    tile_col = part * (columns // TILE) + wide * 2 + across
                    slot = slot_ref[tile_row * COL_TILES + tile_col]
                    rating = rating_ref[0, jnp.maximum(slot, 0)].astype(jnp.float32)
                    piece = predicted[down * TILE:(down + 1) * TILE, across * TILE:(across + 1) * TILE]
                    piece = jnp.where(slot >= 0, piece - rating, 0.0).astype(jnp.bfloat16)
                    residual[
                        tile_row * TILE:(tile_row + 1) * TILE,
                        wide * WIDE + across * TILE:wide * WIDE + (across + 1) * TILE,
                    ] = piece
        item_grad = lax.dot_general(
            residual[:, cols], users_ref[...], contract_first, preferred_element_type=jnp.float32
        )
        held = panel_ref[cols, :]
        new_ref[cols, :] = held - learn_rate * (item_grad + weight_decay * held)
    for block in range(ROW_TILES // 2):
        rows = slice(block * WIDE, (block + 1) * WIDE)
        user_part = jnp.dot(residual[rows, :], rounded[...], preferred_element_type=jnp.float32)
        if has_total:
            user_part = total_ref[rows, :] + user_part
        out_ref[rows, :] = user_part
    if split:
        core = lax.axis_index("item") % 2
        for index in range(ROW_TILES // 2):
            for ref, own in ((mine_ref, core), (theirs_ref, 1 - core)):
                start = pl.multiple_of((2 * index + own) * TILE, TILE)
                ref[index] = out_ref[pl.ds(start, TILE), :]


def chunk_step(step, part, parts, ids, counts, users, panel, whole_panel, ratings, total, placed):
    columns = COL_TILES * TILE // parts
    split = step == STEPS - 1 and part == parts - 1
    has_total = total is not None
    smem = pl.BlockSpec(memory_space=pltpu.SMEM)

    def whole(shape):
        return pl.BlockSpec(shape, lambda i: (0,) * len(shape))

    where = part if whole_panel else 0
    operands = [ids, counts, users, panel, ratings]
    in_specs = [
        smem,
        smem,
        whole(users.shape),
        pl.BlockSpec((columns, R), lambda i: (where, 0)),
        pl.BlockSpec((1, SLOTS, TILE, TILE), lambda i: (step, 0, 0, 0)),
    ]
    aliases = {}
    rows_shape = (ROW_TILES * TILE, R)
    if has_total:
        if not split:
            aliases[len(operands)] = 1
        operands.append(total)
        in_specs.append(whole(rows_shape))
    if step == STEPS - 1:
        new_shape = jax.ShapeDtypeStruct((COL_TILES * TILE, R), jnp.float32)
        new_spec = pl.BlockSpec((columns, R), lambda i: (part, 0))
        if part > 0:
            aliases[len(operands)] = 0
            operands.append(placed)
            in_specs.append(pl.BlockSpec(memory_space=pl.ANY))
    else:
        new_shape = jax.ShapeDtypeStruct((columns, R), jnp.float32)
        new_spec = whole((columns, R))
    scratch = [
        pltpu.SMEM((ROW_TILES * COL_TILES,), jnp.int32),
        pltpu.VMEM((ROW_TILES * TILE, columns), jnp.bfloat16),
        pltpu.VMEM((columns, R), jnp.bfloat16),
    ]
    if split:
        half = (ROW_TILES // 2, TILE, R)
        out_shape = (new_shape,) + (jax.ShapeDtypeStruct(half, jnp.float32),) * 2
        out_specs = (new_spec, whole(half), whole(half))
        scratch.append(pltpu.VMEM(rows_shape, jnp.float32))
    else:
        out_shape = (new_shape, jax.ShapeDtypeStruct(rows_shape, jnp.float32))
        out_specs = (new_spec, whole(rows_shape))
    flops = 3 * 2 * ROW_TILES * TILE * columns * R
    return pl.pallas_call(
        functools.partial(chunk_body, step, part, parts, has_total, split),
        grid=(1,),
        in_specs=in_specs,
        out_specs=out_specs,
        out_shape=out_shape,
        scratch_shapes=scratch,
        input_output_aliases=aliases,
        cost_estimate=pl.CostEstimate(flops=flops, bytes_accessed=4 << 20, transcendentals=0),
        name="chunk_%d_%d" % (step, part),
    )(*operands)


def shards(user_factors, item_panels, ratings, tile_ids, tile_count):
    parts = 2
    ids = tile_ids.reshape(STEPS, SLOTS)
    counts = tile_count.reshape(STEPS, 1)
    pieces = [item_panels] * parts
    total = None
    placed = None
    for step in range(STEPS):
        moved = []
        for part in range(parts):
            results = chunk_step(
                step, part, parts, ids, counts, user_factors, pieces[part], step == 0, ratings, total, placed
            )
            if step == STEPS - 1:
                placed = results[0]
            else:
                moved.append(passed_along(results[0], "user", 1))
            total = results[1]
        pieces = moved
    mine, theirs = results[1], results[2]
    pairs = [(source, source ^ 1) for source in range(lax.axis_size("item"))]
    joined = mine + lax.ppermute(theirs, "item", pairs)
    spread = lax.all_to_all(joined, "item", 0, 0, axis_index_groups=CORE_GROUPS)
    share_grad = jnp.sum(spread, axis=0) * user_scale
    return (placed, share_grad)


def solution(mesh):
    in_specs = (
        P("user", None),
        P(("user", "item"), None),
        P(None, "user", "item", None),
        P(None, "user", "item"),
        P(None, "user", "item"),
    )
    out_specs = (P(("user", "item"), None), P(("user", "item"), None))
    return jax.shard_map(shards, mesh=mesh, in_specs=in_specs, out_specs=out_specs, check_vma=False)
```

```python
import functools

import jax
import jax.numpy as jnp
from jax import lax
from jax.experimental import pallas as pl
from jax.experimental.pallas import tpu as pltpu
from jax.sharding import PartitionSpec as P

R = 256
TILE = 128
STEPS = 3
ROW_TILES = 8
COL_TILES = 8
SLOTS = 24
ROWS = ROW_TILES * TILE
COLS = COL_TILES * TILE
WIDE = 2 * TILE
HALF = COLS // 2


learn_rate = 0.05
weight_decay = 0.02
user_scale = 1.0 / 64.0

CORE_GROUPS = [[0, 2, 4, 6], [1, 3, 5, 7]]

smem = pl.BlockSpec(memory_space=pltpu.SMEM)
vmem = pl.BlockSpec(memory_space=pltpu.VMEM)
anywhere = pl.BlockSpec(memory_space=pl.ANY)
contract_last = (((1,), (1,)), ((), ()))
contract_first = (((0,), (0,)), ((), ()))


def passed_along(value, axis, steps):
    count = lax.axis_size(axis)
    pairs = [(source, (source + steps) % count) for source in range(count)]
    return lax.ppermute(value, axis, pairs)


def find_slots(step, first_col, ids_ref, count_ref, slot_ref):
    for tile in range(ROW_TILES * COL_TILES):
        slot_ref[tile] = -1
    live_count = count_ref[0, 0, step]
    for slot in range(SLOTS):
        slot_ref[ids_ref[step, 0, slot]] = jnp.where(slot < live_count, slot, -1)


def fill_residual(first_col, users_ref, rounded_ref, rating_at, slot_ref, residual_ref, before_ratings=None):
    for wide in range(HALF // WIDE):
        cols = slice(wide * WIDE, (wide + 1) * WIDE)
        for block in range(ROWS // WIDE):
            rows = slice(block * WIDE, (block + 1) * WIDE)
            predicted = lax.dot_general(
                users_ref[rows, :], rounded_ref[cols, :], contract_last, preferred_element_type=jnp.float32
            )
            if before_ratings is not None:
                before_ratings()
                before_ratings = None
            for down in range(2):
                for across in range(2):
                    tile_row = block * 2 + down
                    tile_col = first_col + wide * 2 + across
                    slot = slot_ref[tile_row * COL_TILES + tile_col]
                    rating = rating_at(jnp.maximum(slot, 0)).astype(jnp.float32)
                    piece = predicted[down * TILE:(down + 1) * TILE, across * TILE:(across + 1) * TILE]
                    piece = jnp.where(slot >= 0, piece - rating, 0.0).astype(jnp.bfloat16)
                    residual_ref[
                        tile_row * TILE:(tile_row + 1) * TILE,
                        wide * WIDE + across * TILE:wide * WIDE + (across + 1) * TILE,
                    ] = piece


def update_panel(users_ref, panel_ref, residual_ref, new_ref):
    for wide in range(HALF // WIDE):
        cols = slice(wide * WIDE, (wide + 1) * WIDE)
        item_grad = lax.dot_general(
            residual_ref[:, cols], users_ref[...], contract_first, preferred_element_type=jnp.float32
        )
        held = panel_ref[cols, :]
        new_ref[cols, :] = held - learn_rate * (item_grad + weight_decay * held)


def first_kernel(ids_ref, count_ref, users_hbm, panel_hbm, rating_hbm, new_ref, residual_ref, rounded_ref,
                 slot_ref, users_ref, panel_ref, rating_ref, users_sem, panel_sem, rating_sem):
    panel_copy = pltpu.make_async_copy(panel_hbm.at[pl.ds(0, HALF)], panel_ref, panel_sem)
    users_copy = pltpu.make_async_copy(users_hbm, users_ref, users_sem)
    rating_copy = pltpu.make_async_copy(rating_hbm.at[0], rating_ref, rating_sem)
    panel_copy.start()
    users_copy.start()
    rating_copy.start()
    find_slots(0, 0, ids_ref, count_ref, slot_ref)
    panel_copy.wait()
    rounded_ref[...] = panel_ref[...].astype(jnp.bfloat16)
    users_copy.wait()
    fill_residual(0, users_ref, rounded_ref, lambda slot: rating_ref[slot], slot_ref, residual_ref, rating_copy.wait)
    update_panel(users_ref, panel_ref, residual_ref, new_ref)


def add_user_part(blocks, total_ref, out_ref):
    for block in range(ROWS // WIDE):
        rows = slice(block * WIDE, (block + 1) * WIDE)
        part = None
        for residual_ref, rounded_ref in blocks:
            term = jnp.dot(residual_ref[rows, :], rounded_ref[...], preferred_element_type=jnp.float32)
            part = term if part is None else part + term
        if total_ref is not None:
            part = part + total_ref[rows, :]
        out_ref[rows, :] = part


def early_kernel(step, ids_ref, count_ref, users_ref, panel_ref, rating_ref, new_ref, residual_ref, rounded_ref,
                 slot_ref):
    find_slots(step, 0, ids_ref, count_ref, slot_ref)
    rounded_ref[...] = panel_ref[...].astype(jnp.bfloat16)
    fill_residual(0, users_ref, rounded_ref, lambda slot: rating_ref[step, slot], slot_ref, residual_ref)
    update_panel(users_ref, panel_ref, residual_ref, new_ref)


def late_kernel(step, *refs):
    refs = list(refs)
    ids_ref, count_ref, users_ref, panel_ref, rating_ref, early_residual, early_rounded = refs[:7]
    total_ref = refs.pop(7) if step > 0 else None
    new_ref, out_ref, slot_ref, residual_ref, rounded_ref = refs[7:]
    if step == 0:
        panel_ref = panel_ref.at[pl.ds(HALF, HALF)]
    find_slots(step, COL_TILES // 2, ids_ref, count_ref, slot_ref)
    rounded_ref[...] = panel_ref[...].astype(jnp.bfloat16)
    fill_residual(
        COL_TILES // 2, users_ref, rounded_ref, lambda slot: rating_ref[step, slot], slot_ref, residual_ref
    )
    update_panel(users_ref, panel_ref, residual_ref, new_ref)
    add_user_part([(early_residual, early_rounded), (residual_ref, rounded_ref)], total_ref, out_ref)


def last_early_kernel(step, ids_ref, count_ref, users_ref, panel_ref, rating_ref, total_ref, new_ref, out_ref,
                      slot_ref, residual_ref, rounded_ref):
    find_slots(step, 0, ids_ref, count_ref, slot_ref)
    rounded_ref[...] = panel_ref[...].astype(jnp.bfloat16)
    fill_residual(0, users_ref, rounded_ref, lambda slot: rating_ref[step, slot], slot_ref, residual_ref)
    update_panel(users_ref, panel_ref, residual_ref, new_ref)
    add_user_part([(residual_ref, rounded_ref)], total_ref, out_ref)


def last_late_kernel(step, ids_ref, count_ref, users_ref, panel_ref, rating_ref, total_ref,
                     residual_ref, mine_ref, theirs_ref, slot_ref, rounded_ref):
    find_slots(step, COL_TILES // 2, ids_ref, count_ref, slot_ref)
    rounded_ref[...] = panel_ref[...].astype(jnp.bfloat16)
    fill_residual(
        COL_TILES // 2, users_ref, rounded_ref, lambda slot: rating_ref[step, slot], slot_ref, residual_ref
    )
    core = lax.axis_index("item") % 2
    for index in range(ROW_TILES // 2):
        for ref, own in ((theirs_ref, 1 - core), (mine_ref, core)):
            rows = pl.ds(pl.multiple_of((2 * index + own) * TILE, TILE), TILE)
            part = jnp.dot(residual_ref[rows, :], rounded_ref[...], preferred_element_type=jnp.float32)
            ref[index] = (part + total_ref[rows, :]) * user_scale


def last_update_kernel(users_ref, panel_ref, residual_ref, placed_ref, new_ref):
    new_ref[:HALF, :] = placed_ref[...]
    update_panel(users_ref, panel_ref, residual_ref, new_ref.at[pl.ds(HALF, HALF)])


panel_half = jax.ShapeDtypeStruct((HALF, R), jnp.float32)
residual_half = jax.ShapeDtypeStruct((ROWS, HALF), jnp.bfloat16)
rounded_half = jax.ShapeDtypeStruct((HALF, R), jnp.bfloat16)
row_sum = jax.ShapeDtypeStruct((ROWS, R), jnp.float32)
quarter_sums = jax.ShapeDtypeStruct((ROW_TILES // 2, TILE, R), jnp.float32)
slot_scratch = pltpu.SMEM((ROW_TILES * COL_TILES,), jnp.int32)
half_scratch = [slot_scratch, pltpu.VMEM((ROWS, HALF), jnp.bfloat16), pltpu.VMEM((HALF, R), jnp.bfloat16)]


def kernel_call(body, name, matmuls, operands, in_specs, out_shape, scratch, aliases=None):
    return pl.pallas_call(
        body,
        in_specs=in_specs,
        out_specs=jax.tree.map(lambda _: vmem, out_shape),
        out_shape=out_shape,
        scratch_shapes=scratch,
        input_output_aliases=aliases or {},
        compiler_params=pltpu.CompilerParams(vmem_limit_bytes=16 << 20),
        cost_estimate=pl.CostEstimate(
            flops=matmuls * 2 * ROWS * HALF * R, bytes_accessed=3 << 20, transcendentals=0
        ),
        name=name,
    )(*operands)


def shards(user_factors, item_panels, ratings, tile_ids, tile_count):
    ids = tile_ids.transpose(0, 2, 1)
    counts = tile_count.transpose(1, 2, 0)
    lists = [pltpu.with_memory_space_constraint(a, pltpu.HBM) for a in (ids, counts)]
    list_specs = [smem, smem]

    new, early_residual, early_rounded = kernel_call(
        first_kernel, "first", 2,
        lists + [pltpu.with_memory_space_constraint(a, pltpu.HBM) for a in (user_factors, item_panels, ratings)],
        list_specs + [anywhere] * 3,
        (panel_half, residual_half, rounded_half),
        [
            slot_scratch,
            pltpu.VMEM((ROWS, R), jnp.bfloat16),
            pltpu.VMEM((HALF, R), jnp.float32),
            pltpu.VMEM((SLOTS, TILE, TILE), jnp.bfloat16),
            pltpu.SemaphoreType.DMA,
            pltpu.SemaphoreType.DMA,
            pltpu.SemaphoreType.DMA,
        ],
    )
    new, user_factors, late_panel, ratings = lax.optimization_barrier((new, user_factors, item_panels, ratings))
    early = passed_along(new, "user", 1)
    total = None
    for step in range(STEPS - 1):
        operands = lists + [user_factors, late_panel, ratings, early_residual, early_rounded]
        aliases = {}
        if step > 0:
            aliases = {len(operands): 1}
            operands.append(total)
        new, total = kernel_call(
            functools.partial(late_kernel, step), "late_%d" % step, 4,
            operands, list_specs + [vmem] * (len(operands) - 2), (panel_half, row_sum), half_scratch, aliases,
        )
        late = passed_along(new, "user", 1)
        step += 1
        if step < STEPS - 1:
            new, early_residual, early_rounded = kernel_call(
                functools.partial(early_kernel, step), "early_%d" % step, 2,
                lists + [user_factors, early, ratings], list_specs + [vmem] * 3,
                (panel_half, residual_half, rounded_half), [slot_scratch],
            )
            early = passed_along(new, "user", 1)
        else:
            placed, total = kernel_call(
                functools.partial(last_early_kernel, step), "early_%d" % step, 3,
                lists + [user_factors, early, ratings, total], list_specs + [vmem] * 4,
                (panel_half, row_sum), half_scratch, {5: 1},
            )
        late_panel = late
    residual, mine, theirs = kernel_call(
        functools.partial(last_late_kernel, STEPS - 1), "late_%d" % (STEPS - 1), 2,
        lists + [user_factors, late_panel, ratings, total], list_specs + [vmem] * 4,
        (residual_half, quarter_sums, quarter_sums), [slot_scratch, pltpu.VMEM((HALF, R), jnp.bfloat16)],
    )
    pairs = [(source, source ^ 1) for source in range(lax.axis_size("item"))]
    received = lax.ppermute(theirs, "item", pairs)
    panels = kernel_call(
        last_update_kernel, "last_update", 1,
        [user_factors, late_panel, residual, placed], [vmem] * 4,
        jax.ShapeDtypeStruct((COLS, R), jnp.float32), [],
    )
    spread = lax.all_to_all(mine + received, "item", 0, 0, axis_index_groups=CORE_GROUPS)
    return (panels, jnp.sum(spread, axis=0))


def solution(mesh):
    in_specs = (
        P("user", None),
        P(("user", "item"), None),
        P(None, "user", "item", None),
        P(None, "user", "item"),
        P(None, "user", "item"),
    )
    out_specs = (P(("user", "item"), None), P(("user", "item"), None))
    return jax.shard_map(shards, mesh=mesh, in_specs=in_specs, out_specs=out_specs, check_vma=False)
```

```python
import functools

import jax
import jax.numpy as jnp
from jax import lax
from jax.experimental import pallas as pl
from jax.experimental.pallas import tpu as pltpu
from jax.sharding import PartitionSpec as P

R = 256
TILE = 128
STEPS = 3
ROW_TILES = 8
COL_TILES = 8
SLOTS = 24
ROWS = ROW_TILES * TILE
COLS = COL_TILES * TILE
WIDE = 2 * TILE
PARTS = ((0, 4), (4, 4))


learn_rate = 0.05
weight_decay = 0.02
user_scale = 1.0 / 64.0

CORE_GROUPS = [[0, 2, 4, 6], [1, 3, 5, 7]]

vmem = pl.BlockSpec(memory_space=pltpu.VMEM)
anywhere = pl.BlockSpec(memory_space=pl.ANY)
contract_last = (((1,), (1,)), ((), ()))
contract_first = (((0,), (0,)), ((), ()))


def passed_along(value, axis, steps):
    count = lax.axis_size(axis)
    pairs = [(source, (source + steps) % count) for source in range(count)]
    return lax.ppermute(value, axis, pairs)


def in_hbm(array):
    return pltpu.with_memory_space_constraint(array, pltpu.HBM)


def start_lists(ids_hbm, count_hbm, ids_ref, count_ref, ids_sem, count_sem):
    copies = [
        pltpu.make_async_copy(ids_hbm, ids_ref, ids_sem),
        pltpu.make_async_copy(count_hbm, count_ref, count_sem),
    ]
    for copy in copies:
        copy.start()
    return copies


def find_slots(step, ids_ref, count_ref, slot_ref):
    for tile in range(ROW_TILES * COL_TILES):
        slot_ref[tile] = -1
    live_count = count_ref[0, 0, step]
    for slot in range(SLOTS):
        slot_ref[ids_ref[step, 0, slot]] = jnp.where(slot < live_count, slot, -1)


def fill_residual(part, users_ref, rounded_ref, rating_ref, slot_ref, residual_ref, before_ratings):
    first_col, tiles = part
    width = min(WIDE, tiles * TILE)
    for wide in range(tiles * TILE // width):
        cols = slice(wide * width, (wide + 1) * width)
        for block in range(ROWS // WIDE):
            rows = slice(block * WIDE, (block + 1) * WIDE)
            predicted = lax.dot_general(
                users_ref[rows, :], rounded_ref[cols, :], contract_last, preferred_element_type=jnp.float32
            )
            if wide == 0 and block == 0:
                before_ratings()
            for down in range(2):
                for across in range(width // TILE):
                    tile_row = block * 2 + down
                    tile_col = first_col + wide * (width // TILE) + across
                    slot = slot_ref[tile_row * COL_TILES + tile_col]
                    rating = rating_ref[jnp.maximum(slot, 0)].astype(jnp.float32)
                    piece = predicted[down * TILE:(down + 1) * TILE, across * TILE:(across + 1) * TILE]
                    piece = jnp.where(slot >= 0, piece - rating, 0.0).astype(jnp.bfloat16)
                    residual_ref[
                        tile_row * TILE:(tile_row + 1) * TILE,
                        wide * width + across * TILE:wide * width + (across + 1) * TILE,
                    ] = piece


def update_panel(part, users_ref, panel_ref, residual_ref, new_ref):
    width = min(WIDE, part[1] * TILE)
    for wide in range(part[1] * TILE // width):
        cols = slice(wide * width, (wide + 1) * width)
        item_grad = lax.dot_general(
            residual_ref[:, cols], users_ref[...], contract_first, preferred_element_type=jnp.float32
        )
        held = panel_ref[cols, :]
        new_ref[cols, :] = held - learn_rate * (item_grad + weight_decay * held)


def first_kernel(part, ids_hbm, count_hbm, users_hbm, panel_hbm, rating_hbm,
                 new_ref, residual_ref, rounded_ref, users_ref, rating_ref,
                 slot_ref, ids_ref, count_ref, ids_sem, count_sem, panel_ref, users_sem, panel_sem, rating_sem):
    lists = start_lists(ids_hbm, count_hbm, ids_ref, count_ref, ids_sem, count_sem)
    panel_copy = pltpu.make_async_copy(
        panel_hbm.at[pl.ds(part[0] * TILE, part[1] * TILE)], panel_ref, panel_sem
    )
    users_copy = pltpu.make_async_copy(users_hbm, users_ref, users_sem)
    rating_copy = pltpu.make_async_copy(rating_hbm.at[0], rating_ref, rating_sem)
    panel_copy.start()
    users_copy.start()
    rating_copy.start()
    for copy in lists:
        copy.wait()
    find_slots(0, ids_ref, count_ref, slot_ref)
    panel_copy.wait()
    rounded_ref[...] = panel_ref[...].astype(jnp.bfloat16)
    users_copy.wait()
    fill_residual(part, users_ref, rounded_ref, rating_ref, slot_ref, residual_ref, rating_copy.wait)
    update_panel(part, users_ref, panel_ref, residual_ref, new_ref)


def opening_kernel(part, prefetch, *refs):
    refs = list(refs)
    ids_hbm, count_hbm, users_ref, panel_hbm, rating_ref = refs[:5]
    del refs[:5]
    rating_hbm = refs.pop(0) if prefetch else None
    new_ref, residual_ref, rounded_ref = refs[:3]
    del refs[:3]
    later_ref = refs.pop(0) if prefetch else None
    slot_ref, ids_ref, count_ref, ids_sem, count_sem, panel_ref, panel_sem = refs[:7]
    lists = start_lists(ids_hbm, count_hbm, ids_ref, count_ref, ids_sem, count_sem)
    panel_copy = pltpu.make_async_copy(
        panel_hbm.at[pl.ds(part[0] * TILE, part[1] * TILE)], panel_ref, panel_sem
    )
    panel_copy.start()
    if prefetch:
        later_copy = pltpu.make_async_copy(rating_hbm.at[pl.ds(1, STEPS - 1)], later_ref, refs[7])
        later_copy.start()
    for copy in lists:
        copy.wait()
    find_slots(0, ids_ref, count_ref, slot_ref)
    panel_copy.wait()
    rounded_ref[...] = panel_ref[...].astype(jnp.bfloat16)
    fill_residual(part, users_ref, rounded_ref, rating_ref, slot_ref, residual_ref, lambda: None)
    update_panel(part, users_ref, panel_ref, residual_ref, new_ref)
    if prefetch:
        later_copy.wait()


def residual_stage(step, part, lists_hbm, users_ref, panel_ref, rating_ref, residual_ref, rounded_ref, scratch):
    slot_ref, ids_ref, count_ref, ids_sem, count_sem = scratch
    lists = start_lists(*lists_hbm, ids_ref, count_ref, ids_sem, count_sem)
    rounded_ref[...] = panel_ref[...].astype(jnp.bfloat16)

    def lists_ready():
        for copy in lists:
            copy.wait()
        find_slots(step, ids_ref, count_ref, slot_ref)

    fill_residual(
        part, users_ref, rounded_ref, rating_ref.at[step - 1], slot_ref, residual_ref, lists_ready
    )


def step_kernel(step, part, ids_hbm, count_hbm, users_ref, panel_ref, rating_ref,
                new_ref, residual_ref, rounded_ref, *scratch):
    residual_stage(
        step, part, (ids_hbm, count_hbm), users_ref, panel_ref, rating_ref, residual_ref, rounded_ref, scratch
    )
    update_panel(part, users_ref, panel_ref, residual_ref, new_ref)


def sum_kernel(count, has_total, *refs):
    blocks = list(zip(refs[:count], refs[count:2 * count]))
    total_ref = refs[2 * count] if has_total else None
    out_ref = refs[-1]
    for block in range(ROWS // WIDE):
        rows = slice(block * WIDE, (block + 1) * WIDE)
        value = total_ref[rows, :] if has_total else None
        for residual_ref, rounded_ref in blocks:
            term = jnp.dot(residual_ref[rows, :], rounded_ref[...], preferred_element_type=jnp.float32)
            value = term if value is None else value + term
        out_ref[rows, :] = value


def share_sums(own, residual_ref, rounded_ref, total_ref, out_ref):
    for index in range(ROW_TILES // 2):
        rows = pl.ds(pl.multiple_of((2 * index + own) * TILE, TILE), TILE)
        term = jnp.dot(residual_ref[rows, :], rounded_ref[...], preferred_element_type=jnp.float32)
        out_ref[index] = (term + total_ref[rows, :]) * user_scale


def last_kernel(step, part, ids_hbm, count_hbm, users_ref, panel_ref, rating_ref, total_ref,
                residual_ref, rounded_ref, theirs_ref, *scratch):
    residual_stage(
        step, part, (ids_hbm, count_hbm), users_ref, panel_ref, rating_ref, residual_ref, rounded_ref, scratch
    )
    core = lax.axis_index("item") % 2
    share_sums(1 - core, residual_ref, rounded_ref, total_ref, theirs_ref)


def finish_kernel(part, count, users_ref, panel_ref, residual_ref, rounded_ref, total_ref, *refs):
    placed_refs = refs[:count]
    mine_ref, new_ref = refs[count:]
    core = lax.axis_index("item") % 2
    share_sums(core, residual_ref, rounded_ref, total_ref, mine_ref)
    for (first_col, tiles), placed_ref in zip(PARTS, placed_refs):
        new_ref[first_col * TILE:(first_col + tiles) * TILE, :] = placed_ref[...]
    update_panel(
        part, users_ref, panel_ref, residual_ref, new_ref.at[pl.ds(part[0] * TILE, part[1] * TILE)]
    )


def floats(*shape):
    return jax.ShapeDtypeStruct(shape, jnp.float32)


def rounded(*shape):
    return jax.ShapeDtypeStruct(shape, jnp.bfloat16)


def part_shapes(part):
    width = part[1] * TILE
    return (floats(width, R), rounded(ROWS, width), rounded(width, R))


LISTS = [
    pltpu.SMEM((ROW_TILES * COL_TILES,), jnp.int32),
    pltpu.SMEM((STEPS, 1, SLOTS), jnp.int32),
    pltpu.SMEM((1, 1, STEPS), jnp.int32),
    pltpu.SemaphoreType.DMA,
    pltpu.SemaphoreType.DMA,
]
ROW_SUM = floats(ROWS, R)
QUARTERS = floats(ROW_TILES // 2, TILE, R)


def kernel_call(body, name, work, operands, in_specs, out_shape, scratch, aliases=None):
    return pl.pallas_call(
        body,
        in_specs=in_specs,
        out_specs=jax.tree.map(lambda _: vmem, out_shape),
        out_shape=out_shape,
        scratch_shapes=scratch,
        input_output_aliases=aliases or {},
        compiler_params=pltpu.CompilerParams(vmem_limit_bytes=16 << 20),
        cost_estimate=pl.CostEstimate(
            flops=work * 2 * ROWS * TILE * R, bytes_accessed=work << 18, transcendentals=0
        ),
        name=name,
    )(*operands)


def shards(user_factors, item_panels, ratings, tile_ids, tile_count):
    lists = [in_hbm(tile_ids.transpose(0, 2, 1)), in_hbm(tile_count.transpose(1, 2, 0))]
    list_specs = [anywhere] * 2
    final = len(PARTS) - 1
    panel_hbm = in_hbm(item_panels)
    rating_hbm = in_hbm(ratings)
    moved = []
    blocks = []
    for index, part in enumerate(PARTS):
        panel_scratch = [pltpu.VMEM((part[1] * TILE, R), jnp.float32)]
        if index == 0:
            new, residual, rounded_part, users, rating_now = kernel_call(
                functools.partial(first_kernel, part), "first", 2 * part[1],
                lists + [in_hbm(user_factors), panel_hbm, rating_hbm], list_specs + [anywhere] * 3,
                part_shapes(part) + (rounded(ROWS, R), rounded(SLOTS, TILE, TILE)),
                LISTS + panel_scratch + [pltpu.SemaphoreType.DMA] * 3,
            )
        else:
            prefetch = index == 1
            operands = lists + [users, panel_hbm, rating_now]
            specs = list_specs + [vmem, anywhere, vmem]
            shapes = part_shapes(part)
            if prefetch:
                operands.append(rating_hbm)
                specs.append(anywhere)
                shapes = shapes + (rounded(STEPS - 1, SLOTS, TILE, TILE),)
            results = kernel_call(
                functools.partial(opening_kernel, part, prefetch), "opening_%d" % index, 2 * part[1],
                operands, specs, shapes, LISTS + panel_scratch + [pltpu.SemaphoreType.DMA] * (1 + prefetch),
            )
            new, residual, rounded_part = results[:3]
            if prefetch:
                rating_later = results[3]
        moved.append(passed_along(new, "user", 1))
        blocks.append((residual, rounded_part))

    def add_parts(name, blocks, total):
        operands = [pair[0] for pair in blocks] + [pair[1] for pair in blocks]
        aliases = {}
        if total is not None:
            aliases = {len(operands): 0}
            operands.append(total)
        return kernel_call(
            functools.partial(sum_kernel, len(blocks), total is not None), name, COL_TILES,
            operands, [vmem] * len(operands), ROW_SUM, [], aliases,
        )

    total = add_parts("sum_0", blocks, None)
    for step in range(1, STEPS):
        pieces, moved, blocks = moved, [], []
        for index, part in enumerate(PARTS):
            if step == STEPS - 1 and index == final:
                break
            new, residual, rounded_part = kernel_call(
                functools.partial(step_kernel, step, part), "step_%d_%d" % (step, index), 2 * part[1],
                lists + [users, pieces[index], rating_later], list_specs + [vmem] * 3,
                part_shapes(part), LISTS,
            )
            moved.append(passed_along(new, "user", 1) if step < STEPS - 1 else new)
            blocks.append((residual, rounded_part))
        total = add_parts("sum_%d" % step, blocks, total)
    part = PARTS[final]
    width = part[1] * TILE
    residual, rounded_part, theirs = kernel_call(
        functools.partial(last_kernel, STEPS - 1, part), "last", 2 * part[1],
        lists + [users, pieces[final], rating_later, total], list_specs + [vmem] * 4,
        (rounded(ROWS, width), rounded(width, R), QUARTERS), LISTS,
    )
    pairs = [(source, source ^ 1) for source in range(lax.axis_size("item"))]
    received = lax.ppermute(theirs, "item", pairs)
    mine, panels = kernel_call(
        functools.partial(finish_kernel, part, final), "finish", 2 * part[1],
        [users, pieces[final], residual, rounded_part, total] + moved, [vmem] * (5 + final),
        (QUARTERS, floats(COLS, R)), [],
    )
    spread = lax.all_to_all(mine + received, "item", 0, 0, axis_index_groups=CORE_GROUPS)
    return (panels, jnp.sum(spread, axis=0))


def solution(mesh):
    in_specs = (
        P("user", None),
        P(("user", "item"), None),
        P(None, "user", "item", None),
        P(None, "user", "item"),
        P(None, "user", "item"),
    )
    out_specs = (P(("user", "item"), None), P(("user", "item"), None))
    return jax.shard_map(shards, mesh=mesh, in_specs=in_specs, out_specs=out_specs, check_vma=False)
```

```python
import functools

import jax
import jax.numpy as jnp
from jax import lax
from jax.experimental import pallas as pl
from jax.experimental.pallas import tpu as pltpu
from jax.sharding import PartitionSpec as P


R = 256
TILE = 128
STEPS = 3
ROW_TILES = 8
COL_TILES = 8
SLOTS = 24
ROWS = ROW_TILES * TILE
COLS = COL_TILES * TILE
WIDE = 2 * TILE
PARTS = ((0, 2), (2, 4), (6, 2))


learn_rate = 0.05
weight_decay = 0.02
user_scale = 1.0 / 64.0

CORE_GROUPS = [[0, 2, 4, 6], [1, 3, 5, 7]]

smem = pl.BlockSpec(memory_space=pltpu.SMEM)
vmem = pl.BlockSpec(memory_space=pltpu.VMEM)
anywhere = pl.BlockSpec(memory_space=pl.ANY)
contract_last = (((1,), (1,)), ((), ()))
contract_first = (((0,), (0,)), ((), ()))


def passed_along(value, axis, steps):
    count = lax.axis_size(axis)
    pairs = [(source, (source + steps) % count) for source in range(count)]
    return lax.ppermute(value, axis, pairs)


def in_hbm(array):
    return pltpu.with_memory_space_constraint(array, pltpu.HBM)


def row_tile(place):
    return 2 * (place % (ROW_TILES // 2)) + place // (ROW_TILES // 2)


def start_lists(ids_hbm, count_hbm, ids_ref, count_ref, ids_sem, count_sem):
    copies = [
        pltpu.make_async_copy(ids_hbm, ids_ref, ids_sem),
        pltpu.make_async_copy(count_hbm, count_ref, count_sem),
    ]
    for copy in copies:
        copy.start()
    return copies


def find_slots(step, ids_ref, count_ref, slot_ref):
    for tile in range(ROW_TILES * COL_TILES):
        slot_ref[tile] = -1
    live_count = count_ref[0, 0, step]
    for slot in range(SLOTS):
        slot_ref[ids_ref[step, 0, slot]] = jnp.where(slot < live_count, slot, -1)


def fill_residual(part, users_ref, rounded_ref, less_rating, residual_ref, before_ratings=None):
    width = min(WIDE, part[1] * TILE)
    for wide in range(part[1] * TILE // width):
        cols = slice(wide * width, (wide + 1) * width)
        for half in range(2):
            predicted = lax.dot_general(
                users_ref[half].reshape(ROWS // 2, R), rounded_ref[cols, :], contract_last,
                preferred_element_type=jnp.float32,
            )
            if before_ratings is not None:
                before_ratings()
                before_ratings = None
            for down in range(ROW_TILES // 2):
                for across in range(width // TILE):
                    rows = slice(down * TILE, (down + 1) * TILE)
                    col = wide * (width // TILE) + across
                    piece = predicted[rows, across * TILE:(across + 1) * TILE]
                    piece = less_rating(piece, half, down, part[0] + col)
                    residual_ref[half, rows, col * TILE:(col + 1) * TILE] = piece.astype(jnp.bfloat16)


def listed_rating(rating_ref, slot_ref):
    def less_rating(piece, half, down, tile_col):
        slot = slot_ref[row_tile(half * (ROW_TILES // 2) + down) * COL_TILES + tile_col]
        rating = rating_ref[jnp.maximum(slot, 0)].astype(jnp.float32)
        return jnp.where(slot >= 0, piece - rating, 0.0)

    return less_rating


def spread_rating(spread_ref):
    def less_rating(piece, half, down, tile_col):
        rating = spread_ref[
            half, down * TILE:(down + 1) * TILE, tile_col * TILE:(tile_col + 1) * TILE
        ].astype(jnp.float32)
        return jnp.where(rating == rating, piece - rating, 0.0)

    return less_rating


def spread_kernel(step, ids_hbm, count_hbm, rating_ref, spread_ref, slot_ref, ids_ref, count_ref, ids_sem, count_sem):
    for copy in start_lists(ids_hbm, count_hbm, ids_ref, count_ref, ids_sem, count_sem):
        copy.wait()
    find_slots(step, ids_ref, count_ref, slot_ref)
    for half in range(2):
        for down in range(ROW_TILES // 2):
            for col in range(COL_TILES):
                slot = slot_ref[row_tile(half * (ROW_TILES // 2) + down) * COL_TILES + col]
                rating = rating_ref[step - 1, jnp.maximum(slot, 0)]
                spread_ref[half, down * TILE:(down + 1) * TILE, col * TILE:(col + 1) * TILE] = jnp.where(
                    slot >= 0, rating, jnp.array(jnp.nan, jnp.bfloat16)
                )


def update_panel(part, users_ref, panel_ref, residual_ref, new_ref):
    width = min(WIDE, part[1] * TILE)
    for wide in range(part[1] * TILE // width):
        cols = slice(wide * width, (wide + 1) * width)
        item_grad = lax.dot_general(
            residual_ref[:, :, cols].reshape(ROWS, width), users_ref[...].reshape(ROWS, R), contract_first,
            preferred_element_type=jnp.float32,
        )
        held = panel_ref[cols, :]
        new_ref[cols, :] = held - learn_rate * (item_grad + weight_decay * held)


def first_kernel(part, ids_hbm, count_hbm, users_hbm, panel_hbm, rating_hbm,
                 new_ref, residual_ref, rounded_ref, users_ref, rating_ref,
                 slot_ref, ids_ref, count_ref, ids_sem, count_sem, panel_ref, users_sem, panel_sem, rating_sem):
    lists = start_lists(ids_hbm, count_hbm, ids_ref, count_ref, ids_sem, count_sem)
    panel_copy = pltpu.make_async_copy(
        panel_hbm.at[pl.ds(part[0] * TILE, part[1] * TILE)], panel_ref, panel_sem
    )
    users_copies = [
        pltpu.make_async_copy(users_hbm.at[:, half], users_ref.at[half], users_sem.at[half]) for half in range(2)
    ]
    rating_copy = pltpu.make_async_copy(rating_hbm.at[0], rating_ref, rating_sem)
    panel_copy.start()
    for copy in users_copies:
        copy.start()
    rating_copy.start()
    for copy in lists:
        copy.wait()
    find_slots(0, ids_ref, count_ref, slot_ref)
    panel_copy.wait()
    rounded_ref[...] = panel_ref[...].astype(jnp.bfloat16)
    users_copies[0].wait()

    def rest_ready():
        users_copies[1].wait()
        rating_copy.wait()

    fill_residual(part, users_ref, rounded_ref, listed_rating(rating_ref, slot_ref), residual_ref, rest_ready)
    update_panel(part, users_ref, panel_ref, residual_ref, new_ref)


def opening_kernel(part, prefetch, *refs):
    refs = list(refs)
    ids_hbm, count_hbm, users_ref, panel_hbm, rating_ref = refs[:5]
    del refs[:5]
    rating_hbm = refs.pop(0) if prefetch else None
    new_ref, residual_ref, rounded_ref = refs[:3]
    del refs[:3]
    later_ref = refs.pop(0) if prefetch else None
    slot_ref, ids_ref, count_ref, ids_sem, count_sem, panel_ref, panel_sem = refs[:7]
    lists = start_lists(ids_hbm, count_hbm, ids_ref, count_ref, ids_sem, count_sem)
    panel_copy = pltpu.make_async_copy(
        panel_hbm.at[pl.ds(part[0] * TILE, part[1] * TILE)], panel_ref, panel_sem
    )
    panel_copy.start()
    if prefetch:
        later_copy = pltpu.make_async_copy(rating_hbm.at[pl.ds(1, STEPS - 1)], later_ref, refs[7])
        later_copy.start()
    for copy in lists:
        copy.wait()
    find_slots(0, ids_ref, count_ref, slot_ref)
    panel_copy.wait()
    rounded_ref[...] = panel_ref[...].astype(jnp.bfloat16)
    fill_residual(part, users_ref, rounded_ref, listed_rating(rating_ref, slot_ref), residual_ref)
    update_panel(part, users_ref, panel_ref, residual_ref, new_ref)
    if prefetch:
        later_copy.wait()


def step_kernel(part, users_ref, panel_ref, spread_ref, new_ref, residual_ref, rounded_ref):
    rounded_ref[...] = panel_ref[...].astype(jnp.bfloat16)
    fill_residual(part, users_ref, rounded_ref, spread_rating(spread_ref), residual_ref)
    update_panel(part, users_ref, panel_ref, residual_ref, new_ref)


def sum_kernel(count, has_total, *refs):
    blocks = list(zip(refs[:count], refs[count:2 * count]))
    total_ref = refs[2 * count] if has_total else None
    out_ref = refs[-1]
    for half in range(2):
        value = total_ref[half] if has_total else None
        for residual_ref, rounded_ref in blocks:
            term = jnp.dot(residual_ref[half], rounded_ref[...], preferred_element_type=jnp.float32)
            value = term if value is None else value + term
        out_ref[half] = value


def share_sums(own, residual_ref, rounded_ref, total_ref, out_ref):
    term = jnp.dot(residual_ref[own], rounded_ref[...], preferred_element_type=jnp.float32)
    out_ref[...] = (term + total_ref[own]) * user_scale


def last_kernel(part, users_ref, panel_ref, spread_ref, total_ref, residual_ref, rounded_ref, theirs_ref):
    rounded_ref[...] = panel_ref[...].astype(jnp.bfloat16)
    fill_residual(part, users_ref, rounded_ref, spread_rating(spread_ref), residual_ref)
    core = lax.axis_index("item") % 2
    share_sums(1 - core, residual_ref, rounded_ref, total_ref, theirs_ref)


def finish_kernel(part, count, users_ref, panel_ref, residual_ref, rounded_ref, total_ref, *refs):
    placed_refs = refs[:count]
    mine_ref, new_ref = refs[count:]
    core = lax.axis_index("item") % 2
    share_sums(core, residual_ref, rounded_ref, total_ref, mine_ref)
    for (first_col, tiles), placed_ref in zip(PARTS, placed_refs):
        new_ref[first_col * TILE:(first_col + tiles) * TILE, :] = placed_ref[...]
    update_panel(
        part, users_ref, panel_ref, residual_ref, new_ref.at[pl.ds(part[0] * TILE, part[1] * TILE)]
    )


def floats(*shape):
    return jax.ShapeDtypeStruct(shape, jnp.float32)


def rounded(*shape):
    return jax.ShapeDtypeStruct(shape, jnp.bfloat16)


def part_shapes(part):
    width = part[1] * TILE
    return (floats(width, R), rounded(2, ROWS // 2, width), rounded(width, R))


USERS = rounded(2, ROW_TILES // 2, TILE, R)
LISTS = [
    pltpu.SMEM((ROW_TILES * COL_TILES,), jnp.int32),
    pltpu.SMEM((STEPS, 1, SLOTS), jnp.int32),
    pltpu.SMEM((1, 1, STEPS), jnp.int32),
    pltpu.SemaphoreType.DMA,
    pltpu.SemaphoreType.DMA,
]
ROW_SUM = floats(2, ROWS // 2, R)
HALF_SUM = floats(ROWS // 2, R)


def kernel_call(body, work, operands, in_specs, out_shape, scratch, aliases=None):
    return pl.pallas_call(
        body,
        in_specs=in_specs,
        out_specs=jax.tree.map(lambda a: smem if a.dtype == jnp.int32 else vmem, out_shape),
        out_shape=out_shape,
        scratch_shapes=scratch,
        input_output_aliases=aliases or {},
        compiler_params=pltpu.CompilerParams(vmem_limit_bytes=16 << 20),
        cost_estimate=pl.CostEstimate(
            flops=work * 2 * ROWS * TILE * R, bytes_accessed=work << 18, transcendentals=0
        ),
    )(*operands)


def one_device(user_factors, item_panels, ratings, tile_ids, tile_count):
    lists = [in_hbm(tile_ids.transpose(0, 2, 1)), in_hbm(tile_count.transpose(1, 2, 0))]
    list_specs = [anywhere] * 2
    final = len(PARTS) - 1
    panel_hbm = in_hbm(item_panels)
    rating_hbm = in_hbm(ratings)
    moved = []
    blocks = []
    for index, part in enumerate(PARTS):
        panel_scratch = [pltpu.VMEM((part[1] * TILE, R), jnp.float32)]
        if index == 0:
            new, residual, rounded_part, users, rating_now = kernel_call(
                functools.partial(first_kernel, part), 2 * part[1],
                lists + [in_hbm(user_factors.reshape(ROW_TILES // 2, 2, TILE, R)), panel_hbm, rating_hbm], list_specs + [anywhere] * 3,
                part_shapes(part) + (USERS, rounded(SLOTS, TILE, TILE)),
                LISTS + panel_scratch + [pltpu.SemaphoreType.DMA((2,))] + [pltpu.SemaphoreType.DMA] * 2,
            )
        else:
            prefetch = index == 1
            operands = lists + [users, panel_hbm, rating_now]
            specs = list_specs + [vmem, anywhere, vmem]
            shapes = part_shapes(part)
            if prefetch:
                operands.append(rating_hbm)
                specs.append(anywhere)
                shapes = shapes + (rounded(STEPS - 1, SLOTS, TILE, TILE),)
            results = kernel_call(
                functools.partial(opening_kernel, part, prefetch), 2 * part[1],
                operands, specs, shapes, LISTS + panel_scratch + [pltpu.SemaphoreType.DMA] * (1 + prefetch),
            )
            new, residual, rounded_part = results[:3]
            if prefetch:
                rating_later = results[3]
        moved.append(passed_along(new, "user", 1))
        blocks.append((residual, rounded_part))

    def add_parts(blocks, total):
        operands = [pair[0] for pair in blocks] + [pair[1] for pair in blocks]
        aliases = {}
        if total is not None:
            aliases = {len(operands): 0}
            operands.append(total)
        return kernel_call(
            functools.partial(sum_kernel, len(blocks), total is not None), COL_TILES,
            operands, [vmem] * len(operands), ROW_SUM, [], aliases,
        )

    total = add_parts(blocks, None)
    spread = [
        kernel_call(
            functools.partial(spread_kernel, step), 2, lists + [rating_later],
            list_specs + [vmem], rounded(2, ROWS // 2, COLS), LISTS,
        )
        for step in range(1, STEPS)
    ]
    for step in range(1, STEPS):
        pieces, moved, blocks = moved, [], []
        for index, part in enumerate(PARTS):
            if step == STEPS - 1 and index == final:
                break
            new, residual, rounded_part = kernel_call(
                functools.partial(step_kernel, part), 2 * part[1],
                [users, pieces[index], spread[step - 1]], [vmem] * 3, part_shapes(part), [],
            )
            if step < STEPS - 1:
                new = passed_along(new, "user", 1)
            moved.append(new)
            blocks.append((residual, rounded_part))
        total = add_parts(blocks, total)
    part = PARTS[final]
    width = part[1] * TILE
    residual, rounded_part, theirs = kernel_call(
        functools.partial(last_kernel, part), 2 * part[1],
        [users, pieces[final], spread[-1], total], [vmem] * 4,
        (rounded(2, ROWS // 2, width), rounded(width, R), HALF_SUM), [],
    )
    pairs = [(source, source ^ 1) for source in range(lax.axis_size("item"))]
    received = lax.ppermute(theirs, "item", pairs)
    mine, panels = kernel_call(
        functools.partial(finish_kernel, part, final), 2 * part[1],
        [users, pieces[final], residual, rounded_part, total] + moved, [vmem] * (5 + final),
        (HALF_SUM, floats(COLS, R)), [],
    )
    joined = (mine + received).reshape(ROW_TILES // 2, TILE, R)
    shares = lax.all_to_all(joined, "item", 0, 0, axis_index_groups=CORE_GROUPS)
    return (panels, jnp.sum(shares, axis=0))


def solution(mesh):
    in_specs = (
        P("user", None),
        P(("user", "item"), None),
        P(None, "user", "item", None),
        P(None, "user", "item"),
        P(None, "user", "item"),
    )
    out_specs = (P(("user", "item"), None), P(("user", "item"), None))
    return jax.shard_map(one_device, mesh=mesh, in_specs=in_specs, out_specs=out_specs, check_vma=False)
```

```python
import functools

import jax
import jax.numpy as jnp
from jax import lax
from jax.experimental import pallas as pl
from jax.experimental.pallas import tpu as pltpu
from jax.sharding import PartitionSpec as P


R = 256
TILE = 128
STEPS = 3
ROW_TILES = 8
COL_TILES = 8
SLOTS = 24
ROWS = ROW_TILES * TILE
COLS = COL_TILES * TILE
WIDE = 2 * TILE
PARTS = ((0, 2), (2, 4), (6, 2))


learn_rate = 0.05
weight_decay = 0.02
user_scale = 1.0 / 64.0

CORE_GROUPS = [[0, 2, 4, 6], [1, 3, 5, 7]]

smem = pl.BlockSpec(memory_space=pltpu.SMEM)
vmem = pl.BlockSpec(memory_space=pltpu.VMEM)
anywhere = pl.BlockSpec(memory_space=pl.ANY)
contract_last = (((1,), (1,)), ((), ()))
contract_first = (((0,), (0,)), ((), ()))


def passed_along(value, axis, steps):
    count = lax.axis_size(axis)
    pairs = [(source, (source + steps) % count) for source in range(count)]
    return lax.ppermute(value, axis, pairs)


def in_hbm(array):
    return pltpu.with_memory_space_constraint(array, pltpu.HBM)


def row_tile(place):
    return 2 * (place % (ROW_TILES // 2)) + place // (ROW_TILES // 2)


def start_lists(ids_hbm, count_hbm, ids_ref, count_ref, ids_sem, count_sem):
    copies = [
        pltpu.make_async_copy(ids_hbm, ids_ref, ids_sem),
        pltpu.make_async_copy(count_hbm, count_ref, count_sem),
    ]
    for copy in copies:
        copy.start()
    return copies


def find_slots(step, ids_ref, count_ref, slot_ref):
    for tile in range(ROW_TILES * COL_TILES):
        slot_ref[tile] = -1
    live_count = count_ref[0, 0, step]
    for slot in range(SLOTS):
        slot_ref[ids_ref[step, 0, slot]] = jnp.where(slot < live_count, slot, -1)


def predict(cols, half, users_ref, rounded_ref):
    return lax.dot_general(
        users_ref[half].reshape(ROWS // 2, R), rounded_ref[cols, :], contract_last, preferred_element_type=jnp.float32
    )


def take_ratings(part, cols, half, predicted, less_rating, residual_ref):
    for down in range(ROW_TILES // 2):
        for col in range(cols.start // TILE, cols.stop // TILE):
            rows = slice(down * TILE, (down + 1) * TILE)
            piece = predicted[rows, col * TILE - cols.start:(col + 1) * TILE - cols.start]
            piece = less_rating(piece, half, down, part[0] + col)
            residual_ref[half, rows, col * TILE:(col + 1) * TILE] = piece.astype(jnp.bfloat16)


def column_blocks(part):
    width = min(WIDE, part[1] * TILE)
    return [slice(start, start + width) for start in range(0, part[1] * TILE, width)]


def fill_residual(part, users_ref, rounded_ref, less_rating, residual_ref):
    for cols in column_blocks(part):
        for half in range(2):
            take_ratings(part, cols, half, predict(cols, half, users_ref, rounded_ref), less_rating, residual_ref)


def listed_rating(rating_ref, slot_ref):
    def less_rating(piece, half, down, tile_col):
        slot = slot_ref[row_tile(half * (ROW_TILES // 2) + down) * COL_TILES + tile_col]
        rating = rating_ref[jnp.maximum(slot, 0)].astype(jnp.float32)
        return jnp.where(slot >= 0, piece - rating, 0.0)

    return less_rating


def spread_rating(spread_ref):
    def less_rating(piece, half, down, tile_col):
        rating = spread_ref[
            half, down * TILE:(down + 1) * TILE, tile_col * TILE:(tile_col + 1) * TILE
        ].astype(jnp.float32)
        return jnp.where(rating == rating, piece - rating, 0.0)

    return less_rating


def spread_kernel(step, ids_hbm, count_hbm, rating_ref, spread_ref, slot_ref, ids_ref, count_ref, ids_sem, count_sem):
    for copy in start_lists(ids_hbm, count_hbm, ids_ref, count_ref, ids_sem, count_sem):
        copy.wait()
    find_slots(step, ids_ref, count_ref, slot_ref)
    for half in range(2):
        for down in range(ROW_TILES // 2):
            for col in range(COL_TILES):
                slot = slot_ref[row_tile(half * (ROW_TILES // 2) + down) * COL_TILES + col]
                rating = rating_ref[step - 1, jnp.maximum(slot, 0)]
                spread_ref[half, down * TILE:(down + 1) * TILE, col * TILE:(col + 1) * TILE] = jnp.where(
                    slot >= 0, rating, jnp.array(jnp.nan, jnp.bfloat16)
                )


def update_panel(part, users_ref, panel_ref, residual_ref, new_ref):
    width = min(WIDE, part[1] * TILE)
    for wide in range(part[1] * TILE // width):
        cols = slice(wide * width, (wide + 1) * width)
        item_grad = lax.dot_general(
            residual_ref[:, :, cols].reshape(ROWS, width), users_ref[...].reshape(ROWS, R), contract_first,
            preferred_element_type=jnp.float32,
        )
        held = panel_ref[cols, :]
        new_ref[cols, :] = held - learn_rate * (item_grad + weight_decay * held)


def first_kernel(part, ids_hbm, count_hbm, users_hbm, panel_hbm, rating_hbm,
                 new_ref, residual_ref, rounded_ref, users_ref, rating_ref,
                 slot_ref, ids_ref, count_ref, ids_sem, count_sem, panel_ref, users_sem, panel_sem, rating_sem):
    lists = start_lists(ids_hbm, count_hbm, ids_ref, count_ref, ids_sem, count_sem)
    panel_copy = pltpu.make_async_copy(
        panel_hbm.at[pl.ds(part[0] * TILE, part[1] * TILE)], panel_ref, panel_sem
    )
    users_copies = [
        pltpu.make_async_copy(users_hbm.at[:, half], users_ref.at[half], users_sem.at[half]) for half in range(2)
    ]
    rating_copy = pltpu.make_async_copy(rating_hbm.at[0], rating_ref, rating_sem)
    panel_copy.start()
    for copy in users_copies:
        copy.start()
    rating_copy.start()
    for copy in lists:
        copy.wait()
    find_slots(0, ids_ref, count_ref, slot_ref)
    panel_copy.wait()
    rounded_ref[...] = panel_ref[...].astype(jnp.bfloat16)
    for copy in users_copies:
        copy.wait()
    places = [(cols, half) for cols in column_blocks(part) for half in range(2)]
    predicted = [predict(cols, half, users_ref, rounded_ref) for cols, half in places]
    rating_copy.wait()
    for (cols, half), values in zip(places, predicted):
        take_ratings(part, cols, half, values, listed_rating(rating_ref, slot_ref), residual_ref)
    update_panel(part, users_ref, panel_ref, residual_ref, new_ref)


def opening_kernel(part, prefetch, *refs):
    refs = list(refs)
    ids_hbm, count_hbm, users_ref, panel_hbm, rating_ref = refs[:5]
    del refs[:5]
    rating_hbm = refs.pop(0) if prefetch else None
    new_ref, residual_ref, rounded_ref = refs[:3]
    del refs[:3]
    later_ref = refs.pop(0) if prefetch else None
    slot_ref, ids_ref, count_ref, ids_sem, count_sem, panel_ref, panel_sem = refs[:7]
    lists = start_lists(ids_hbm, count_hbm, ids_ref, count_ref, ids_sem, count_sem)
    panel_copy = pltpu.make_async_copy(
        panel_hbm.at[pl.ds(part[0] * TILE, part[1] * TILE)], panel_ref, panel_sem
    )
    panel_copy.start()
    if prefetch:
        later_copy = pltpu.make_async_copy(rating_hbm.at[pl.ds(1, STEPS - 1)], later_ref, refs[7])
        later_copy.start()
    for copy in lists:
        copy.wait()
    find_slots(0, ids_ref, count_ref, slot_ref)
    panel_copy.wait()
    rounded_ref[...] = panel_ref[...].astype(jnp.bfloat16)
    fill_residual(part, users_ref, rounded_ref, listed_rating(rating_ref, slot_ref), residual_ref)
    update_panel(part, users_ref, panel_ref, residual_ref, new_ref)
    if prefetch:
        later_copy.wait()


def step_kernel(part, users_ref, panel_ref, spread_ref, new_ref, residual_ref, rounded_ref):
    rounded_ref[...] = panel_ref[...].astype(jnp.bfloat16)
    fill_residual(part, users_ref, rounded_ref, spread_rating(spread_ref), residual_ref)
    update_panel(part, users_ref, panel_ref, residual_ref, new_ref)


def sum_kernel(count, has_total, *refs):
    blocks = list(zip(refs[:count], refs[count:2 * count]))
    total_ref = refs[2 * count] if has_total else None
    out_ref = refs[-1]
    for half in range(2):
        value = total_ref[half] if has_total else None
        for residual_ref, rounded_ref in blocks:
            term = jnp.dot(residual_ref[half], rounded_ref[...], preferred_element_type=jnp.float32)
            value = term if value is None else value + term
        out_ref[half] = value


def share_sums(own, residual_ref, rounded_ref, total_ref, out_ref):
    term = jnp.dot(residual_ref[own], rounded_ref[...], preferred_element_type=jnp.float32)
    out_ref[...] = (term + total_ref[own]) * user_scale


def last_kernel(part, users_ref, panel_ref, spread_ref, total_ref, residual_ref, rounded_ref, theirs_ref):
    rounded_ref[...] = panel_ref[...].astype(jnp.bfloat16)
    fill_residual(part, users_ref, rounded_ref, spread_rating(spread_ref), residual_ref)
    core = lax.axis_index("item") % 2
    share_sums(1 - core, residual_ref, rounded_ref, total_ref, theirs_ref)


def finish_kernel(part, count, users_ref, panel_ref, residual_ref, rounded_ref, total_ref, *refs):
    placed_refs = refs[:count]
    mine_ref, new_ref = refs[count:]
    core = lax.axis_index("item") % 2
    share_sums(core, residual_ref, rounded_ref, total_ref, mine_ref)
    for (first_col, tiles), placed_ref in zip(PARTS, placed_refs):
        new_ref[first_col * TILE:(first_col + tiles) * TILE, :] = placed_ref[...]
    update_panel(
        part, users_ref, panel_ref, residual_ref, new_ref.at[pl.ds(part[0] * TILE, part[1] * TILE)]
    )


def floats(*shape):
    return jax.ShapeDtypeStruct(shape, jnp.float32)


def rounded(*shape):
    return jax.ShapeDtypeStruct(shape, jnp.bfloat16)


def part_shapes(part):
    width = part[1] * TILE
    return (floats(width, R), rounded(2, ROWS // 2, width), rounded(width, R))


USERS = rounded(2, ROW_TILES // 2, TILE, R)
LISTS = [
    pltpu.SMEM((ROW_TILES * COL_TILES,), jnp.int32),
    pltpu.SMEM((STEPS, 1, SLOTS), jnp.int32),
    pltpu.SMEM((1, 1, STEPS), jnp.int32),
    pltpu.SemaphoreType.DMA,
    pltpu.SemaphoreType.DMA,
]
ROW_SUM = floats(2, ROWS // 2, R)
HALF_SUM = floats(ROWS // 2, R)


def kernel_call(body, work, operands, in_specs, out_shape, scratch, aliases=None):
    return pl.pallas_call(
        body,
        in_specs=in_specs,
        out_specs=jax.tree.map(lambda a: smem if a.dtype == jnp.int32 else vmem, out_shape),
        out_shape=out_shape,
        scratch_shapes=scratch,
        input_output_aliases=aliases or {},
        compiler_params=pltpu.CompilerParams(vmem_limit_bytes=16 << 20),
        cost_estimate=pl.CostEstimate(
            flops=work * 2 * ROWS * TILE * R, bytes_accessed=work << 18, transcendentals=0
        ),
    )(*operands)


def one_device(user_factors, item_panels, ratings, tile_ids, tile_count):
    lists = [in_hbm(tile_ids.transpose(0, 2, 1)), in_hbm(tile_count.transpose(1, 2, 0))]
    list_specs = [anywhere] * 2
    final = len(PARTS) - 1
    panel_hbm = in_hbm(item_panels)
    rating_hbm = in_hbm(ratings)
    moved = []
    blocks = []
    for index, part in enumerate(PARTS):
        panel_scratch = [pltpu.VMEM((part[1] * TILE, R), jnp.float32)]
        if index == 0:
            new, residual, rounded_part, users, rating_now = kernel_call(
                functools.partial(first_kernel, part), 2 * part[1],
                lists + [in_hbm(user_factors.reshape(ROW_TILES // 2, 2, TILE, R)), panel_hbm, rating_hbm], list_specs + [anywhere] * 3,
                part_shapes(part) + (USERS, rounded(SLOTS, TILE, TILE)),
                LISTS + panel_scratch + [pltpu.SemaphoreType.DMA((2,))] + [pltpu.SemaphoreType.DMA] * 2,
            )
        else:
            prefetch = index == 1
            operands = lists + [users, panel_hbm, rating_now]
            specs = list_specs + [vmem, anywhere, vmem]
            shapes = part_shapes(part)
            if prefetch:
                operands.append(rating_hbm)
                specs.append(anywhere)
                shapes = shapes + (rounded(STEPS - 1, SLOTS, TILE, TILE),)
            results = kernel_call(
                functools.partial(opening_kernel, part, prefetch), 2 * part[1],
                operands, specs, shapes, LISTS + panel_scratch + [pltpu.SemaphoreType.DMA] * (1 + prefetch),
            )
            new, residual, rounded_part = results[:3]
            if prefetch:
                rating_later = results[3]
        moved.append(passed_along(new, "user", 1))
        blocks.append((residual, rounded_part))

    def add_parts(blocks, total):
        operands = [pair[0] for pair in blocks] + [pair[1] for pair in blocks]
        aliases = {}
        if total is not None:
            aliases = {len(operands): 0}
            operands.append(total)
        return kernel_call(
            functools.partial(sum_kernel, len(blocks), total is not None), COL_TILES,
            operands, [vmem] * len(operands), ROW_SUM, [], aliases,
        )

    total = add_parts(blocks, None)
    spread = [
        kernel_call(
            functools.partial(spread_kernel, step), 2, lists + [rating_later],
            list_specs + [vmem], rounded(2, ROWS // 2, COLS), LISTS,
        )
        for step in range(1, STEPS)
    ]
    for step in range(1, STEPS):
        pieces, moved, blocks = moved, [], []
        for index, part in enumerate(PARTS):
            if step == STEPS - 1 and index == final:
                break
            new, residual, rounded_part = kernel_call(
                functools.partial(step_kernel, part), 2 * part[1],
                [users, pieces[index], spread[step - 1]], [vmem] * 3, part_shapes(part), [],
            )
            if step < STEPS - 1:
                new = passed_along(new, "user", 1)
            moved.append(new)
            blocks.append((residual, rounded_part))
        total = add_parts(blocks, total)
    part = PARTS[final]
    width = part[1] * TILE
    residual, rounded_part, theirs = kernel_call(
        functools.partial(last_kernel, part), 2 * part[1],
        [users, pieces[final], spread[-1], total], [vmem] * 4,
        (rounded(2, ROWS // 2, width), rounded(width, R), HALF_SUM), [],
    )
    pairs = [(source, source ^ 1) for source in range(lax.axis_size("item"))]
    received = lax.ppermute(theirs, "item", pairs)
    mine, panels = kernel_call(
        functools.partial(finish_kernel, part, final), 2 * part[1],
        [users, pieces[final], residual, rounded_part, total] + moved, [vmem] * (5 + final),
        (HALF_SUM, floats(COLS, R)), [],
    )
    joined = (mine + received).reshape(ROW_TILES // 2, TILE, R)
    shares = lax.all_to_all(joined, "item", 0, 0, axis_index_groups=CORE_GROUPS)
    return (panels, jnp.sum(shares, axis=0))


def solution(mesh):
    in_specs = (
        P("user", None),
        P(("user", "item"), None),
        P(None, "user", "item", None),
        P(None, "user", "item"),
        P(None, "user", "item"),
    )
    out_specs = (P(("user", "item"), None), P(("user", "item"), None))
    return jax.shard_map(one_device, mesh=mesh, in_specs=in_specs, out_specs=out_specs, check_vma=False)
```

```python
import functools

import jax
import jax.numpy as jnp
from jax import lax
from jax.experimental import pallas as pl
from jax.experimental.pallas import tpu as pltpu
from jax.sharding import PartitionSpec as P


R = 256
TILE = 128
STEPS = 3
ROW_TILES = 8
COL_TILES = 8
SLOTS = 24
ROWS = ROW_TILES * TILE
COLS = COL_TILES * TILE
WIDE = 2 * TILE
PARTS = ((0, 2), (2, 4), (6, 2))


learn_rate = 0.05
weight_decay = 0.02
user_scale = 1.0 / 64.0

CORE_GROUPS = [[0, 2, 4, 6], [1, 3, 5, 7]]

smem = pl.BlockSpec(memory_space=pltpu.SMEM)
vmem = pl.BlockSpec(memory_space=pltpu.VMEM)
anywhere = pl.BlockSpec(memory_space=pl.ANY)
contract_last = (((1,), (1,)), ((), ()))
contract_first = (((0,), (0,)), ((), ()))


def passed_along(value, axis, steps):
    count = lax.axis_size(axis)
    pairs = [(source, (source + steps) % count) for source in range(count)]
    return lax.ppermute(value, axis, pairs)


def in_hbm(array):
    return pltpu.with_memory_space_constraint(array, pltpu.HBM)


def row_tile(place):
    return 2 * (place % (ROW_TILES // 2)) + place // (ROW_TILES // 2)


def start_lists(ids_hbm, count_hbm, ids_ref, count_ref, ids_sem, count_sem):
    copies = [
        pltpu.make_async_copy(ids_hbm, ids_ref, ids_sem),
        pltpu.make_async_copy(count_hbm, count_ref, count_sem),
    ]
    for copy in copies:
        copy.start()
    return copies


def find_slots(step, ids_ref, count_ref, slot_ref):
    for tile in range(ROW_TILES * COL_TILES):
        slot_ref[tile] = -1
    live_count = count_ref[0, 0, step]
    for slot in range(SLOTS):
        slot_ref[ids_ref[step, 0, slot]] = jnp.where(slot < live_count, slot, -1)


def predict(cols, half, users_ref, rounded_ref):
    return lax.dot_general(
        users_ref[half].reshape(ROWS // 2, R), rounded_ref[cols, :], contract_last, preferred_element_type=jnp.float32
    )


def take_ratings(part, cols, half, predicted, less_rating, residual_ref):
    for down in range(ROW_TILES // 2):
        for col in range(cols.start // TILE, cols.stop // TILE):
            rows = slice(down * TILE, (down + 1) * TILE)
            piece = predicted[rows, col * TILE - cols.start:(col + 1) * TILE - cols.start]
            piece = less_rating(piece, half, down, part[0] + col)
            residual_ref[half, rows, col * TILE:(col + 1) * TILE] = piece.astype(jnp.bfloat16)


def column_blocks(part):
    width = min(WIDE, part[1] * TILE)
    return [slice(start, start + width) for start in range(0, part[1] * TILE, width)]


def fill_residual(part, users_ref, rounded_ref, less_rating, residual_ref):
    for cols in column_blocks(part):
        for half in range(2):
            take_ratings(part, cols, half, predict(cols, half, users_ref, rounded_ref), less_rating, residual_ref)


def listed_rating(rating_ref, slot_ref):
    def less_rating(piece, half, down, tile_col):
        slot = slot_ref[row_tile(half * (ROW_TILES // 2) + down) * COL_TILES + tile_col]
        rating = rating_ref[jnp.maximum(slot, 0)].astype(jnp.float32)
        return jnp.where(slot >= 0, piece - rating, 0.0)

    return less_rating


def spread_rating(spread_ref):
    def less_rating(piece, half, down, tile_col):
        rating = spread_ref[
            half, down * TILE:(down + 1) * TILE, tile_col * TILE:(tile_col + 1) * TILE
        ].astype(jnp.float32)
        return jnp.where(rating == rating, piece - rating, 0.0)

    return less_rating


def spread_kernel(step, ids_hbm, count_hbm, rating_ref, spread_ref, slot_ref, ids_ref, count_ref, ids_sem, count_sem):
    for copy in start_lists(ids_hbm, count_hbm, ids_ref, count_ref, ids_sem, count_sem):
        copy.wait()
    find_slots(step, ids_ref, count_ref, slot_ref)
    for half in range(2):
        for down in range(ROW_TILES // 2):
            for col in range(COL_TILES):
                slot = slot_ref[row_tile(half * (ROW_TILES // 2) + down) * COL_TILES + col]
                rating = rating_ref[step - 1, jnp.maximum(slot, 0)]
                spread_ref[half, down * TILE:(down + 1) * TILE, col * TILE:(col + 1) * TILE] = jnp.where(
                    slot >= 0, rating, jnp.array(jnp.nan, jnp.bfloat16)
                )


def update_panel(part, users_ref, panel_ref, residual_ref, new_ref):
    width = min(WIDE, part[1] * TILE)
    for wide in range(part[1] * TILE // width):
        cols = slice(wide * width, (wide + 1) * width)
        item_grad = lax.dot_general(
            residual_ref[:, :, cols].reshape(ROWS, width), users_ref[...].reshape(ROWS, R), contract_first,
            preferred_element_type=jnp.float32,
        )
        held = panel_ref[cols, :]
        new_ref[cols, :] = held - learn_rate * (item_grad + weight_decay * held)


def first_kernel(part, ids_hbm, count_hbm, users_hbm, panel_hbm, rating_hbm,
                 new_ref, residual_ref, rounded_ref, users_ref, rating_ref,
                 slot_ref, ids_ref, count_ref, ids_sem, count_sem, panel_ref, users_sem, panel_sem, rating_sem):
    lists = start_lists(ids_hbm, count_hbm, ids_ref, count_ref, ids_sem, count_sem)
    panel_copy = pltpu.make_async_copy(
        panel_hbm.at[pl.ds(part[0] * TILE, part[1] * TILE)], panel_ref, panel_sem
    )
    users_copies = [
        pltpu.make_async_copy(users_hbm.at[:, half], users_ref.at[half], users_sem.at[half]) for half in range(2)
    ]
    rating_copy = pltpu.make_async_copy(rating_hbm.at[0], rating_ref, rating_sem)
    panel_copy.start()
    for copy in users_copies:
        copy.start()
    rating_copy.start()
    for copy in lists:
        copy.wait()
    find_slots(0, ids_ref, count_ref, slot_ref)
    panel_copy.wait()
    rounded_ref[...] = panel_ref[...].astype(jnp.bfloat16)
    for copy in users_copies:
        copy.wait()
    places = [(cols, half) for cols in column_blocks(part) for half in range(2)]
    predicted = [predict(cols, half, users_ref, rounded_ref) for cols, half in places]
    rating_copy.wait()
    for (cols, half), values in zip(places, predicted):
        take_ratings(part, cols, half, values, listed_rating(rating_ref, slot_ref), residual_ref)
    update_panel(part, users_ref, panel_ref, residual_ref, new_ref)


def opening_kernel(part, prefetch, *refs):
    refs = list(refs)
    ids_hbm, count_hbm, users_ref, panel_hbm, rating_ref = refs[:5]
    del refs[:5]
    rating_hbm = refs.pop(0) if prefetch else None
    new_ref, residual_ref, rounded_ref = refs[:3]
    del refs[:3]
    later_ref = refs.pop(0) if prefetch else None
    slot_ref, ids_ref, count_ref, ids_sem, count_sem, panel_ref, panel_sem = refs[:7]
    lists = start_lists(ids_hbm, count_hbm, ids_ref, count_ref, ids_sem, count_sem)
    panel_copy = pltpu.make_async_copy(
        panel_hbm.at[pl.ds(part[0] * TILE, part[1] * TILE)], panel_ref, panel_sem
    )
    panel_copy.start()
    if prefetch:
        later_copy = pltpu.make_async_copy(rating_hbm.at[pl.ds(1, STEPS - 1)], later_ref, refs[7])
        later_copy.start()
    for copy in lists:
        copy.wait()
    find_slots(0, ids_ref, count_ref, slot_ref)
    panel_copy.wait()
    rounded_ref[...] = panel_ref[...].astype(jnp.bfloat16)
    fill_residual(part, users_ref, rounded_ref, listed_rating(rating_ref, slot_ref), residual_ref)
    update_panel(part, users_ref, panel_ref, residual_ref, new_ref)
    if prefetch:
        later_copy.wait()


def step_kernel(part, users_ref, panel_ref, spread_ref, new_ref, residual_ref, rounded_ref):
    rounded_ref[...] = panel_ref[...].astype(jnp.bfloat16)
    fill_residual(part, users_ref, rounded_ref, spread_rating(spread_ref), residual_ref)
    update_panel(part, users_ref, panel_ref, residual_ref, new_ref)


def sum_kernel(count, has_total, *refs):
    blocks = list(zip(refs[:count], refs[count:2 * count]))
    total_ref = refs[2 * count] if has_total else None
    out_ref = refs[-1]
    for half in range(2):
        value = total_ref[half] if has_total else None
        for residual_ref, rounded_ref in blocks:
            term = jnp.dot(residual_ref[half], rounded_ref[...], preferred_element_type=jnp.float32)
            value = term if value is None else value + term
        out_ref[half] = value


def share_sums(own, residual_ref, rounded_ref, total_ref, out_ref):
    term = jnp.dot(residual_ref[own], rounded_ref[...], preferred_element_type=jnp.float32)
    out_ref[...] = (term + total_ref[own]) * user_scale


def last_kernel(part, users_ref, panel_ref, spread_ref, total_ref, residual_ref, rounded_ref, theirs_ref):
    rounded_ref[...] = panel_ref[...].astype(jnp.bfloat16)
    fill_residual(part, users_ref, rounded_ref, spread_rating(spread_ref), residual_ref)
    core = lax.axis_index("item") % 2
    share_sums(1 - core, residual_ref, rounded_ref, total_ref, theirs_ref)


def finish_kernel(part, count, users_ref, panel_ref, residual_ref, rounded_ref, total_ref, *refs):
    placed_refs = refs[:count]
    mine_ref, new_ref = refs[count:]
    core = lax.axis_index("item") % 2
    share_sums(core, residual_ref, rounded_ref, total_ref, mine_ref)
    for (first_col, tiles), placed_ref in zip(PARTS, placed_refs):
        new_ref[first_col * TILE:(first_col + tiles) * TILE, :] = placed_ref[...]
    update_panel(
        part, users_ref, panel_ref, residual_ref, new_ref.at[pl.ds(part[0] * TILE, part[1] * TILE)]
    )


def add_shares(shares_ref, out_ref):
    out_ref[...] = (shares_ref[0] + shares_ref[1]) + (shares_ref[2] + shares_ref[3])


def floats(*shape):
    return jax.ShapeDtypeStruct(shape, jnp.float32)


def rounded(*shape):
    return jax.ShapeDtypeStruct(shape, jnp.bfloat16)


def part_shapes(part):
    width = part[1] * TILE
    return (floats(width, R), rounded(2, ROWS // 2, width), rounded(width, R))


USERS = rounded(2, ROW_TILES // 2, TILE, R)
LISTS = [
    pltpu.SMEM((ROW_TILES * COL_TILES,), jnp.int32),
    pltpu.SMEM((STEPS, 1, SLOTS), jnp.int32),
    pltpu.SMEM((1, 1, STEPS), jnp.int32),
    pltpu.SemaphoreType.DMA,
    pltpu.SemaphoreType.DMA,
]
ROW_SUM = floats(2, ROWS // 2, R)
HALF_SUM = floats(ROWS // 2, R)


def kernel_call(body, work, operands, in_specs, out_shape, scratch, aliases=None):
    return pl.pallas_call(
        body,
        in_specs=in_specs,
        out_specs=jax.tree.map(lambda a: smem if a.dtype == jnp.int32 else vmem, out_shape),
        out_shape=out_shape,
        scratch_shapes=scratch,
        input_output_aliases=aliases or {},
        compiler_params=pltpu.CompilerParams(vmem_limit_bytes=16 << 20),
        cost_estimate=pl.CostEstimate(
            flops=work * 2 * ROWS * TILE * R, bytes_accessed=work << 18, transcendentals=0
        ),
    )(*operands)


def one_device(user_factors, item_panels, ratings, tile_ids, tile_count):
    lists = [in_hbm(tile_ids.transpose(0, 2, 1)), in_hbm(tile_count.transpose(1, 2, 0))]
    list_specs = [anywhere] * 2
    final = len(PARTS) - 1
    panel_hbm = in_hbm(item_panels)
    rating_hbm = in_hbm(ratings)
    moved = []
    blocks = []
    for index, part in enumerate(PARTS):
        panel_scratch = [pltpu.VMEM((part[1] * TILE, R), jnp.float32)]
        if index == 0:
            new, residual, rounded_part, users, rating_now = kernel_call(
                functools.partial(first_kernel, part), 2 * part[1],
                lists + [in_hbm(user_factors.reshape(ROW_TILES // 2, 2, TILE, R)), panel_hbm, rating_hbm], list_specs + [anywhere] * 3,
                part_shapes(part) + (USERS, rounded(SLOTS, TILE, TILE)),
                LISTS + panel_scratch + [pltpu.SemaphoreType.DMA((2,))] + [pltpu.SemaphoreType.DMA] * 2,
            )
        else:
            prefetch = index == 1
            operands = lists + [users, panel_hbm, rating_now]
            specs = list_specs + [vmem, anywhere, vmem]
            shapes = part_shapes(part)
            if prefetch:
                operands.append(rating_hbm)
                specs.append(anywhere)
                shapes = shapes + (rounded(STEPS - 1, SLOTS, TILE, TILE),)
            results = kernel_call(
                functools.partial(opening_kernel, part, prefetch), 2 * part[1],
                operands, specs, shapes, LISTS + panel_scratch + [pltpu.SemaphoreType.DMA] * (1 + prefetch),
            )
            new, residual, rounded_part = results[:3]
            if prefetch:
                rating_later = results[3]
        moved.append(passed_along(new, "user", 1))
        blocks.append((residual, rounded_part))

    def add_parts(blocks, total):
        operands = [pair[0] for pair in blocks] + [pair[1] for pair in blocks]
        aliases = {}
        if total is not None:
            aliases = {len(operands): 0}
            operands.append(total)
        return kernel_call(
            functools.partial(sum_kernel, len(blocks), total is not None), COL_TILES,
            operands, [vmem] * len(operands), ROW_SUM, [], aliases,
        )

    total = add_parts(blocks, None)
    spread = [
        kernel_call(
            functools.partial(spread_kernel, step), 2, lists + [rating_later],
            list_specs + [vmem], rounded(2, ROWS // 2, COLS), LISTS,
        )
        for step in range(1, STEPS)
    ]
    for step in range(1, STEPS):
        pieces, moved, blocks = moved, [], []
        for index, part in enumerate(PARTS):
            if step == STEPS - 1 and index == final:
                break
            new, residual, rounded_part = kernel_call(
                functools.partial(step_kernel, part), 2 * part[1],
                [users, pieces[index], spread[step - 1]], [vmem] * 3, part_shapes(part), [],
            )
            if step < STEPS - 1:
                new = passed_along(new, "user", 1)
            moved.append(new)
            blocks.append((residual, rounded_part))
        total = add_parts(blocks, total)
    part = PARTS[final]
    width = part[1] * TILE
    residual, rounded_part, theirs = kernel_call(
        functools.partial(last_kernel, part), 2 * part[1],
        [users, pieces[final], spread[-1], total], [vmem] * 4,
        (rounded(2, ROWS // 2, width), rounded(width, R), HALF_SUM), [],
    )
    pairs = [(source, source ^ 1) for source in range(lax.axis_size("item"))]
    received = lax.ppermute(theirs, "item", pairs)
    mine, panels = kernel_call(
        functools.partial(finish_kernel, part, final), 2 * part[1],
        [users, pieces[final], residual, rounded_part, total] + moved, [vmem] * (5 + final),
        (HALF_SUM, floats(COLS, R)), [],
    )
    joined = (mine + received).reshape(ROW_TILES // 2, TILE, R)
    shares = lax.all_to_all(joined, "item", 0, 0, axis_index_groups=CORE_GROUPS)
    share_grad = kernel_call(add_shares, 1, [shares], [vmem], floats(TILE, R), [])
    return (panels, share_grad)


def solution(mesh):
    in_specs = (
        P("user", None),
        P(("user", "item"), None),
        P(None, "user", "item", None),
        P(None, "user", "item"),
        P(None, "user", "item"),
    )
    out_specs = (P(("user", "item"), None), P(("user", "item"), None))
    return jax.shard_map(one_device, mesh=mesh, in_specs=in_specs, out_specs=out_specs, check_vma=False)
```
